256 devices in a mesh: dom: 64 (over z, x, core), inst: 4 (over y).
Axes of the slice: x: 4, y: 4, z: 8, core: 2. Of those that a mesh axis runs over, the one named last changes fastest.
Arguments:
- state: float32 [5, 16, 32768], P(None, 'inst', 'dom'), may hold values from -0.65 to 3.75, as said below
- cell_volume: float32 [32768], P('dom'), may hold values from 1 to 4
- step_size: float32 [32768], P('dom'), may hold values from 0.02 to 0.1
- face_normal: float32 [3, 131072], P(None, 'dom'), may hold values from -1 to 1
- owner_arm: float32 [3, 131072], P(None, 'dom'), may hold values from -0.09 to 0.09
- neighbor_arm: float32 [3, 131072], P(None, 'dom'), may hold values from -0.09 to 0.09
- face_owner: int32 [131072], P('dom'), may hold values from 0 to 511, as said below
- face_neighbor: int32 [131072], P('dom'), may hold values from 0 to 767, as said below
- face_count: int32 [64], P('dom'), may hold values from 1024 to 2048, as said below
- send_cells: int32 [256, 64], P('dom'), may hold values from 0 to 511
Outputs:
- new_state: float32 [5, 16, 32768], P(None, 'inst', 'dom')
- residual: float32 [5, 16, 32768], P(None, 'inst', 'dom')
The draws below stay inside these ranges and needn't reach their ends.
Inputs may be any that keep to these rules, and one draw needn't show every extreme that they name: The state is physical: density 0.7 to 1.3 and pressure 0.4 (E - |m|^2 / (2 rho)) 0.7 to 1.3. `face_owner`: local ids of cells of the face's own partition. `face_neighbor`: either a local cell id below 512, or the ghost id 512 + k * 64 + s of block k; blocks of partitions that do not exist are never named. `face_count`: live face slots come first in each partition; some partition has all 2048 slots live. `send_cells`: row 4 q + k lists cells of partition q that fill ghost block k of partition q - o_k, o = (-2, -1, 1, 2); slots that no face names are padding.
All inputs are finite; a program needn't handle non-finite values.
Results may differ from the reference program's by a relative error of at most 0.0003.
Values sent between devices are 32-bit elements; how exact they have to be, the bound alone decides.
No kernel may reach another device: no remote copies, remote signals or barrier semaphores. Data moves between devices by JAX's collectives and lax.ppermute only.
A program may use at most 128 MiB of HBM per device.

```python
import math
import jax
import jax.numpy as jnp
from jax import lax

NVAR = 5
INST = 16
C_DEV = 512
SLOTS = 64
F_DEV = 2048
CELLS = 32768
FACES = 131072
LISTS = 256


HEAT_RATIO = 1.4


PEER_OFFSETS = (-2, -1, 1, 2)


def ghost_counts(key):
    partitions = FACES // F_DEV
    counts = jax.random.randint(jax.random.fold_in(key, 21), (partitions, 4), SLOTS // 2, SLOTS + 1)
    return counts.at[2, 3].set(SLOTS)


def draw_state(key, part):
    grid_shape = (INST, CELLS)
    subkeys = jax.random.split(jax.random.fold_in(key, 51), 3)
    density = jax.random.uniform(subkeys[0], grid_shape, jnp.float32, 0.85, 1.15)
    velocity = jnp.clip(0.25 * jax.random.normal(subkeys[1], (3,) + grid_shape, jnp.float32), -0.5, 0.5)
    pressure = jax.random.uniform(subkeys[2], grid_shape, jnp.float32, 0.85, 1.15)
    momentum = density * velocity
    energy = pressure / (HEAT_RATIO - 1.0) + 0.5 * density * jnp.sum(velocity * velocity, axis=0)
    return jnp.concatenate([density[None], momentum, energy[None]], axis=0).astype(jnp.float32)


def draw_face_owner(key, part):
    partitions = FACES // F_DEV
    owners = jax.random.randint(jax.random.fold_in(key, 11), (partitions, F_DEV), 0, C_DEV)
    owners = owners.at[0, 0].set(C_DEV - 1).at[0, 1].set(0)
    return owners.reshape(FACES).astype(jnp.int32)


def draw_face_neighbor(key, part):
    partitions = FACES // F_DEV
    counts = ghost_counts(key)
    owned_id = jax.random.randint(jax.random.fold_in(key, 31), (partitions, F_DEV), 0, C_DEV)
    choose = jax.random.randint(jax.random.fold_in(key, 32), (partitions, F_DEV), 0, 8)
    slot_draw = jax.random.randint(jax.random.fold_in(key, 33), (partitions, F_DEV), 0, SLOTS)
    receiver = jnp.arange(partitions, dtype=jnp.int32)[:, None]
    offsets = jnp.array(PEER_OFFSETS, dtype=jnp.int32)
    block_index = jnp.minimum(choose, 3)
    source = receiver + offsets[block_index]
    present = (source >= 0) & (source < partitions) & (choose < 4)
    slot_limit = counts[jnp.clip(source, 0, partitions - 1), block_index]
    slot_index = slot_draw % slot_limit
    ghost_id = C_DEV + block_index * SLOTS + slot_index
    result = jnp.where(present, ghost_id, owned_id)
    result = result.at[0, 0].set(0).at[0, 2].set(C_DEV + 4 * SLOTS - 1)
    return result.reshape(FACES).astype(jnp.int32)


def draw_face_count(key, part):
    partitions = FACES // F_DEV
    counts = jax.random.randint(jax.random.fold_in(key, 41), (partitions,), F_DEV // 2, F_DEV + 1)
    fullest = jax.random.randint(jax.random.fold_in(key, 42), (), 0, partitions)
    return counts.at[fullest].set(F_DEV).astype(jnp.int32)


def touch_ends(drawn, own_key, smallest, largest):
    index_at = [jax.random.randint(jax.random.fold_in(own_key, axis), (), 0, length) for axis, length in enumerate(drawn.shape)]
    main_axis = drawn.shape.index(max(drawn.shape))
    neighbour = index_at[:main_axis] + [(index_at[main_axis] + 1) % drawn.shape[main_axis]] + index_at[main_axis + 1:]
    return drawn.at[tuple(index_at)].set(smallest).at[tuple(neighbour)].set(largest)


def levels(own_key, shape, cuts, smallest, largest):
    factor_of = 1.0
    for dim, parts in cuts:
        heights = jax.random.uniform(jax.random.fold_in(jax.random.fold_in(own_key, 6), dim), (parts,), jnp.float32, smallest / len(cuts), largest / len(cuts))
        factor_of = factor_of * jnp.repeat(jnp.exp(heights), shape[dim] // parts).reshape((-1,) + (1,) * (len(shape) - 1 - dim))
    return factor_of


def scatter_about(rng, shape, deviation, reach, cuts=(), held_as=jnp.bfloat16):
    values = jax.random.normal(rng, shape, jnp.float32) * deviation
    if len(cuts) > 0:
        values = levels(rng, shape, cuts, -0.22, 0.18) * values
    return jnp.clip(values, min=-reach, max=reach).astype(held_as)


def setup_inputs(seed: int = 0) -> dict:
    key_list = jax.random.split(jax.random.key(seed), 11)
    state = draw_state(jax.random.fold_in(key_list[10], 71), 0)
    cell_volume = jnp.clip(jnp.exp(math.log(4.0) - 1.3862944 * jax.random.uniform(key_list[1], (CELLS,), jnp.float32) ** levels(key_list[1], (CELLS,), ((0, 64),), -0.2, 0.2)), 1.0, 4.0)
    step_size = jnp.clip(jnp.exp(math.log(0.1) - 1.609438 * jax.random.uniform(key_list[2], (CELLS,), jnp.float32) ** levels(key_list[2], (CELLS,), ((0, 64),), -0.2, 0.2)), 0.02, 0.1)
    face_normal = scatter_about(key_list[3], (3, FACES), 0.4, 1.0, ((1, 64),), jnp.float32)
    owner_arm = scatter_about(key_list[4], (3, FACES), 0.03, 0.09, ((1, 64),), jnp.float32)
    neighbor_arm = scatter_about(key_list[5], (3, FACES), 0.03, 0.09, ((1, 64),), jnp.float32)
    face_owner = draw_face_owner(jax.random.fold_in(key_list[10], 71), 0)
    face_neighbor = draw_face_neighbor(jax.random.fold_in(key_list[10], 71), 0)
    face_count = draw_face_count(jax.random.fold_in(key_list[10], 71), 0)
    send_cells = touch_ends(jax.random.randint(key_list[9], (LISTS, SLOTS), 0, C_DEV), jax.random.fold_in(key_list[9], 1), 0, C_DEV - 1).astype(jnp.int32)
    return {"state": state, "cell_volume": cell_volume, "step_size": step_size, "face_normal": face_normal, "owner_arm": owner_arm, "neighbor_arm": neighbor_arm, "face_owner": face_owner, "face_neighbor": face_neighbor, "face_count": face_count, "send_cells": send_cells}


HEAT_RATIO = 1.4
FREQUENCY = 0.5
PEER_OFFSETS = (-2, -1, 1, 2)

def spectral_table(points):
    indices = jnp.arange(points, dtype=jnp.int32)
    distance = indices[:, None] - indices[None, :]
    nonzero = jnp.where(distance == 0, 1, distance)
    signs = jnp.where(distance % 2 == 0, 1.0, -1.0)
    entries = 0.5 * signs / jnp.tan(jnp.pi * nonzero.astype(jnp.float32) / points)
    return jnp.where(distance == 0, 0.0, entries).astype(jnp.float32)

def extend_field(by_partition, partition, send_rows):
    partitions = by_partition.shape[-2]
    blocks = [jnp.take(by_partition, partition, axis=-2)]
    for position, offset in enumerate(PEER_OFFSETS):
        source = partition + offset
        present = ((source >= 0) & (source < partitions)).astype(by_partition.dtype)
        clipped = jnp.clip(source, 0, partitions - 1).astype(jnp.int32)
        send_row = send_rows[clipped, position]
        ghost_block = jnp.take(jnp.take(by_partition, clipped, axis=-2), send_row, axis=-1)
        blocks.append(ghost_block * present)
    return jnp.concatenate(blocks, axis=-1)

def cell_gradient(extended, owners, neighbors, live_mask, normals, volume):
    cell_total = volume.shape[0]
    left_state = jnp.take(extended, owners, axis=-1)
    right_state = jnp.take(extended, neighbors, axis=-1)
    half_jump = 0.5 * (right_state - left_state) * live_mask
    face_flow = half_jump[None] * normals[:, None, None, :]
    summed = jnp.zeros(face_flow.shape[:-1] + (cell_total,), face_flow.dtype)
    summed = summed.at[..., owners].add(face_flow)
    summed = summed.at[..., neighbors].add(face_flow, mode='drop')
    return summed / volume

def euler_flux(conserved, normals):
    density = conserved[0]
    momentum = conserved[1:4]
    velocity = momentum / density
    pressure = (HEAT_RATIO - 1.0) * (conserved[4] - 0.5 * lax.optimization_barrier(jnp.sum(momentum * velocity, axis=0)))
    normal_speed = lax.optimization_barrier(jnp.sum(velocity * normals[:, None, :], axis=0))
    face_area = jnp.sqrt(lax.optimization_barrier(jnp.sum(normals * normals, axis=0)))
    face_flux = jnp.concatenate([(density * normal_speed)[None], momentum * normal_speed + pressure * normals[:, None, :], ((conserved[4] + pressure) * normal_speed)[None]], axis=0)
    sound_speed = jnp.sqrt(HEAT_RATIO * pressure / density)
    return (face_flux, jnp.abs(normal_speed) + sound_speed * face_area)

def flux_residual(extended, ext_grad, owners, neighbors, live_mask, normals, owner_arm, neighbor_arm, volume):
    cell_total = volume.shape[0]
    left_state = jnp.take(extended, owners, axis=-1) + lax.optimization_barrier(jnp.sum(jnp.take(ext_grad, owners, axis=-1) * owner_arm[:, None, None, :], axis=0))
    right_state = jnp.take(extended, neighbors, axis=-1) + lax.optimization_barrier(jnp.sum(jnp.take(ext_grad, neighbors, axis=-1) * neighbor_arm[:, None, None, :], axis=0))
    flux_left, speed_left = euler_flux(left_state, normals)
    flux_right, speed_right = euler_flux(right_state, normals)
    wave_speed = jnp.maximum(speed_left, speed_right)
    face_flux = (0.5 * (flux_left + flux_right) - 0.5 * wave_speed * (right_state - left_state)) * live_mask
    summed = jnp.zeros(face_flux.shape[:-1] + (cell_total,), face_flux.dtype)
    summed = summed.at[..., owners].add(face_flux)
    summed = summed.at[..., neighbors].add(-face_flux, mode='drop')
    return summed / volume

def reference(state, cell_volume, step_size, face_normal, owner_arm, neighbor_arm, face_owner, face_neighbor, face_count, send_cells):
    owners = face_owner.reshape(-1, F_DEV)
    neighbors = face_neighbor.reshape(-1, F_DEV)
    normals = face_normal.reshape(3, -1, F_DEV)
    owner_arms = owner_arm.reshape(3, -1, F_DEV)
    neighbor_arms = neighbor_arm.reshape(3, -1, F_DEV)
    volumes = cell_volume.reshape(-1, C_DEV)
    send_rows = send_cells.reshape(-1, 4, SLOTS)
    partitions = volumes.shape[0]
    numbers = jnp.arange(partitions, dtype=jnp.int32)
    face_index = jnp.arange(F_DEV, dtype=jnp.int32)

    def section_residual(current):
        by_partition = current.reshape(NVAR, INST, partitions, C_DEV)

        def live_of(partition):
            return (face_index < face_count[partition]).astype(current.dtype)

        def partition_gradient(partition):
            extended = extend_field(by_partition, partition, send_rows)
            return cell_gradient(extended, owners[partition], neighbors[partition], live_of(partition), normals[:, partition], volumes[partition])
        gradients = lax.map(partition_gradient, numbers)
        grad_parts = jnp.moveaxis(gradients, 0, -2)

        def partition_residual(partition):
            extended = extend_field(by_partition, partition, send_rows)
            ext_grad = extend_field(grad_parts, partition, send_rows)
            return flux_residual(extended, ext_grad, owners[partition], neighbors[partition], live_of(partition), normals[:, partition], owner_arms[:, partition], neighbor_arms[:, partition], volumes[partition])
        spatial = lax.map(partition_residual, numbers)
        spatial = jnp.moveaxis(spatial, 0, -2).reshape(NVAR, INST, CELLS)
        derivative = spectral_table(INST).astype(current.dtype)
        source_term = jnp.einsum('ij,vjc->vic', derivative, current, precision=lax.Precision.HIGHEST)
        return spatial + FREQUENCY * source_term
    section_state = state - 0.5 * step_size * section_residual(state)
    residual = section_residual(section_state)
    new_state = state - step_size * residual
    return (new_state, residual)
```

```python
import functools

import jax
import jax.numpy as jnp
import numpy as np
from jax import lax
from jax.experimental import pallas as pl
from jax.experimental.pallas import tpu as pltpu
from jax.sharding import PartitionSpec as P

HEAT_RATIO = 1.4
FREQUENCY = 0.5
NV = 5
CELLS = 512
GHOSTS = 256
FACES = 2048
CHUNK = 512
VROWS = 40
GROWS = 120
BF = jnp.bfloat16
F32 = jnp.float32


def top_rows(shape):
    return (lax.broadcasted_iota(jnp.int32, shape, 0) & 7) < 4


def swap_halves(x):
    return pltpu.roll(x, 4, 0)


def fold(x):
    return x + swap_halves(x)


def pieces(x):
    high = x.astype(BF).astype(F32)
    return jnp.where(top_rows(x.shape), high, x - high).astype(BF)


def matmul(a, b):
    return jnp.dot(a, b, preferred_element_type=F32)


def matmul_t(a, b):
    return lax.dot_general(a, b, (((1,), (1,)), ((), ())), preferred_element_type=F32)


def one_hot(ids, rows):
    cell = lax.broadcasted_iota(jnp.int32, (rows, ids.shape[1]), 0)
    return jnp.where(cell == ids, 1.0, 0.0).astype(F32)


def paired(groups):
    out = []
    for j in range(0, len(groups), 2):
        first = groups[j]
        second = groups[min(j + 1, len(groups) - 1)]
        out.append(jnp.where(top_rows(first.shape), first, second))
    return jnp.concatenate(out, axis=0)


def unpaired(x, count):
    out = []
    for g in range(count):
        block = x[(g // 2) * 8 : (g // 2) * 8 + 8]
        turned = swap_halves(block)
        top = top_rows(block.shape)
        out.append(jnp.where(top, block, turned) if g % 2 == 0 else jnp.where(top, turned, block))
    return jnp.concatenate(out, axis=0)


def send_hot(send):
    return jnp.concatenate([one_hot(send[k : k + 1, :], CELLS) for k in range(4)], axis=1).astype(BF)


def write_messages(table, send, parity, near_ref, far_ref):
    listed = matmul(table, send_hot(send))
    groups = [fold(listed[8 * g : 8 * g + 8]) for g in range(listed.shape[0] // 8)]
    packed = paired(groups)
    up, down = packed[:, :128], packed[:, 128:]
    even = parity == 0
    near_ref[...] = jnp.where(even, up, down)
    far_ref[...] = jnp.where(even, down, up)


def ghost_table(near, cross, relay, parity, count):
    rows = near.shape[0]
    first, second = cross[:rows], cross[rows:]
    low = lax.broadcasted_iota(jnp.int32, (rows, 128), 1) < 64
    even = parity == 0
    left = jnp.where(low, jnp.where(even, second, relay), jnp.where(even, first, near))
    right = jnp.where(low, jnp.where(even, near, first), jnp.where(even, relay, second))
    return pieces(unpaired(jnp.concatenate([left, right], axis=1), count))


def send_kernel(parity_ref, state_ref, send_ref, near_ref, far_ref, wide_ref, dense_ref):
    for v in range(NV):
        wide_ref[8 * v : 8 * v + 4, :] = state_ref[v]
        wide_ref[8 * v + 4 : 8 * v + 8, :] = state_ref[v]
    wide = wide_ref[...]
    write_messages(pieces(wide), send_ref[...], parity_ref[0], near_ref, far_ref)
    dense_ref[...] = paired([wide[8 * v : 8 * v + 8] for v in range(NV)])


def gradient_kernel(
    parity_ref, count_ref, wide_ref, near_in, cross_in, relay_in, owner_ref, neighbor_ref, normal_ref,
    volume_ref, send_ref, table_ref, near_ref, far_ref,
):
    parity = parity_ref[0]
    ghosts = ghost_table(near_in[...], cross_in[...], relay_in[...], parity, NV)
    values = jnp.concatenate([pieces(wide_ref[...]), ghosts], axis=1)
    total = jnp.zeros((GROWS, CELLS), F32)
    for f in range(0, FACES, CHUNK):
        own = one_hot(owner_ref[:, f : f + CHUNK], CELLS)
        other = one_hot(neighbor_ref[:, f : f + CHUNK], CELLS + GHOSTS)
        local = other[:CELLS]
        jump_hot = jnp.concatenate([local - own, other[CELLS:]], axis=0).astype(BF)
        sum_hot = (local + own).astype(BF)
        jump = matmul(values, jump_hot)
        jumps = [fold(jump[8 * v : 8 * v + 8]) for v in range(NV)]
        live = lax.broadcasted_iota(jnp.int32, (1, CHUNK), 1) + f < count_ref[0]
        flows = []
        for d in range(3):
            half = jnp.where(live, 0.5 * normal_ref[d : d + 1, f : f + CHUNK], 0.0)
            for v in range(NV):
                flows.append(jumps[v] * half)
        total = total + matmul_t(pieces(jnp.concatenate(flows, axis=0)), sum_hot)
    inverse = 1.0 / volume_ref[...]
    gradient = jnp.concatenate([fold(total[8 * g : 8 * g + 8]) * inverse for g in range(3 * NV)], axis=0)
    table = pieces(gradient)
    table_ref[...] = table
    write_messages(table, send_ref[...], parity, near_ref, far_ref)


def spatial_groups(
    parity_ref, count_ref, wide_ref, near_in, cross_in, relay_in, table_ref, gnear_in, gcross_in, grelay_in,
    owner_ref, neighbor_ref, normal_ref, owner_arm_ref, neighbor_arm_ref, volume_ref,
):
    parity = parity_ref[0]
    ghosts = ghost_table(near_in[...], cross_in[...], relay_in[...], parity, NV)
    grad_ghosts = ghost_table(gnear_in[...], gcross_in[...], grelay_in[...], parity, 3 * NV)
    local = jnp.concatenate([pieces(wide_ref[...]), table_ref[...]], axis=0)
    values = jnp.concatenate([local, jnp.concatenate([ghosts, grad_ghosts], axis=0)], axis=1)
    total = jnp.zeros((VROWS, CELLS), F32)
    top = top_rows((8, CHUNK))
    sign = jnp.where(top, 1.0, -1.0)
    for f in range(0, FACES, CHUNK):
        own = one_hot(owner_ref[:, f : f + CHUNK], CELLS)
        other = one_hot(neighbor_ref[:, f : f + CHUNK], CELLS + GHOSTS)
        difference = (own - other[:CELLS]).astype(BF)
        left = matmul(local, own.astype(BF))
        right = matmul(values, other.astype(BF))
        live = lax.broadcasted_iota(jnp.int32, (1, CHUNK), 1) + f < count_ref[0]
        normals = [jnp.where(live, normal_ref[d : d + 1, f : f + CHUNK], 0.0) for d in range(3)]
        area = jnp.sqrt(normals[0] * normals[0] + normals[1] * normals[1] + normals[2] * normals[2])
        states = []
        for v in range(NV):
            a, b = left[8 * v : 8 * v + 8], right[8 * v : 8 * v + 8]
            for d in range(3):
                g = VROWS + 8 * (NV * d + v)
                a = a + left[g : g + 8] * owner_arm_ref[d : d + 1, f : f + CHUNK]
                b = b + right[g : g + 8] * neighbor_arm_ref[d : d + 1, f : f + CHUNK]
            states.append(jnp.where(top, a, b) + swap_halves(jnp.where(top, b, a)))
        density, energy = states[0], states[4]
        momentum = states[1:4]
        inverse = 1.0 / density
        velocity = [m * inverse for m in momentum]
        kinetic = momentum[0] * velocity[0] + momentum[1] * velocity[1] + momentum[2] * velocity[2]
        pressure = (HEAT_RATIO - 1.0) * (energy - 0.5 * kinetic)
        speed = velocity[0] * normals[0] + velocity[1] * normals[1] + velocity[2] * normals[2]
        wave = jnp.abs(speed) + jnp.sqrt(HEAT_RATIO * pressure * inverse) * area
        wave = jnp.maximum(wave, swap_halves(wave)) * sign
        flux = [density * speed]
        for d in range(3):
            flux.append(momentum[d] * speed + pressure * normals[d])
        flux.append((energy + pressure) * speed)
        faces = [fold(0.5 * (flux[v] + wave * states[v])) for v in range(NV)]
        total = total + matmul_t(pieces(jnp.concatenate(faces, axis=0)), difference)
    inverse = 1.0 / volume_ref[...]
    return [fold(total[8 * v : 8 * v + 8]) * inverse for v in range(NV)]


def middle_kernel(*refs):
    *common, spectral_ref, step_ref, send_ref, wide_out, dense_ref, near_ref, far_ref = refs
    spatial = spatial_groups(*common)
    wide_ref, parity = common[2], common[0][0]
    groups = []
    for v in range(NV):
        rows = slice(8 * v, 8 * v + 8)
        groups.append(wide_ref[rows] - 0.5 * step_ref[...] * (spatial[v] + spectral_ref[rows]))
    wide = jnp.concatenate(groups, axis=0)
    wide_out[...] = wide
    dense_ref[...] = paired(groups)
    write_messages(pieces(wide), send_ref[...], parity, near_ref, far_ref)


def last_kernel(*refs):
    *common, spectral_ref, step_ref, state_ref, new_ref, residual_ref = refs
    spatial = spatial_groups(*common)
    for v in range(NV):
        rate = (spatial[v] + spectral_ref[8 * v : 8 * v + 8])[:4]
        residual_ref[v] = rate
        new_ref[v] = state_ref[v] - step_ref[...] * rate


def spectral_kernel(index_ref, matrix_ref, mine_ref, next_ref, rest_ref, out_ref):
    matrix = matrix_ref[index_ref[0]]
    data = jnp.concatenate([mine_ref[...], next_ref[...], rest_ref[...]], axis=0)
    m_high, d_high = matrix.astype(BF), data.astype(BF)
    m_low, d_low = (matrix - m_high.astype(F32)).astype(BF), (data - d_high.astype(F32)).astype(BF)
    out_ref[...] = matmul(m_high, d_high) + matmul(m_high, d_low) + matmul(m_low, d_high)


def spectral_matrices(groups, size):
    points = groups * size
    distance = np.arange(points)[:, None] - np.arange(points)[None, :]
    safe = np.where(distance == 0, 1, distance)
    table = 0.5 * np.where(distance % 2 == 0, 1.0, -1.0) / np.tan(np.pi * safe / points)
    table = np.where(distance == 0, 0.0, table) * FREQUENCY
    out = np.zeros((groups, VROWS, groups * 24), np.float32)
    for y in range(groups):
        for v in range(NV):
            for s in range(8):
                for b in range(groups):
                    for t in range(size):
                        column = b * 24 + (v // 2) * 8 + (v % 2) * 4 + t
                        out[y, 8 * v + s, column] = table[size * y + s % size, size * (y ^ b) + t]
    return out


def call(kernel, outputs, scalars, arrays, name):
    smem = pl.BlockSpec(memory_space=pltpu.SMEM)
    vmem = pl.BlockSpec(memory_space=pltpu.VMEM)
    return pl.pallas_call(
        kernel,
        out_shape=[jax.ShapeDtypeStruct(s, d) for s, d in outputs],
        in_specs=[smem] * len(scalars) + [vmem] * len(arrays),
        out_specs=[vmem] * len(outputs),
        compiler_params=pltpu.CompilerParams(vmem_limit_bytes=32 << 20),
        name=name,
    )(*scalars, *arrays)


def local(
    state, cell_volume, step_size, face_normal, owner_arm, neighbor_arm, face_owner, face_neighbor, face_count,
    send_cells,
):
    parts = lax.axis_size("dom")
    place = lax.axis_index("dom")
    parity = (place & 1).astype(jnp.int32).reshape(1)
    line = lax.axis_index("inst").astype(jnp.int32).reshape(1)
    volume = cell_volume.reshape(1, CELLS)
    step = step_size.reshape(1, CELLS)
    owner = face_owner.reshape(1, FACES)
    neighbor = face_neighbor.reshape(1, FACES)
    matrices = jnp.asarray(spectral_matrices(lax.axis_size("inst"), state.shape[1]))
    inside = [(i, i ^ 1) for i in range(parts)]
    across = [(i, i + 1) for i in range(1, parts - 1, 2)] + [(i + 1, i) for i in range(1, parts - 1, 2)]

    def exchange(near, far):
        got = lax.ppermute(near, "dom", inside)
        cross = lax.ppermute(jnp.concatenate([far, got], axis=0), "dom", across)
        relay = lax.ppermute(cross[: far.shape[0]], "dom", inside)
        return got, cross, relay

    def instances(dense):
        one = lax.ppermute(dense, "inst", [(i, i ^ 1) for i in range(4)])
        two = lax.ppermute(jnp.concatenate([dense, one], axis=0), "inst", [(i, i ^ 2) for i in range(4)])
        return call(spectral_kernel, [((VROWS, CELLS), F32)], [line], [matrices, dense, one, two], "spectral")[0]

    def message(rows):
        return [((rows, 128), F32)] * 2

    wide_shape, dense_shape = ((VROWS, CELLS), F32), ((24, CELLS), F32)
    geometry = [owner, neighbor, face_normal]
    arms = [owner_arm, neighbor_arm, volume]
    near, far, wide, dense = call(
        send_kernel, message(24) + [wide_shape, dense_shape], [parity], [state, send_cells], "send"
    )
    for section in range(2):
        ghosts = exchange(near, far)
        spectral = instances(dense)
        table, gnear, gfar = call(
            gradient_kernel, [((GROWS, CELLS), BF)] + message(64), [parity, face_count],
            [wide, *ghosts, *geometry, volume, send_cells], "gradient",
        )
        gradient_ghosts = exchange(gnear, gfar)
        common = [wide, *ghosts, table, *gradient_ghosts, *geometry, *arms, spectral, step]
        if section == 0:
            wide, dense, near, far = call(
                middle_kernel, [wide_shape, dense_shape] + message(24), [parity, face_count], [*common, send_cells],
                "middle",
            )
    shape = state.shape
    return tuple(call(last_kernel, [(shape, F32)] * 2, [parity, face_count], [*common, state], "last"))


def solution(mesh):
    placed = (
        P(None, "inst", "dom"), P("dom"), P("dom"), P(None, "dom"), P(None, "dom"), P(None, "dom"), P("dom"), P("dom"),
        P("dom"), P("dom", None),
    )
    return jax.shard_map(
        local, mesh=mesh, in_specs=placed, out_specs=(P(None, "inst", "dom"), P(None, "inst", "dom")), check_vma=False,
    )
```

```python
import jax
import jax.numpy as jnp
import numpy as np
from jax import lax
from jax.experimental import pallas as pl
from jax.experimental.pallas import tpu as pltpu
from jax.sharding import PartitionSpec as P


HEAT_RATIO = 1.4
FREQUENCY = 0.5
NV = 5
CELLS = 512
GHOSTS = 256
FACES = 2048
CHUNK = 512
VROWS = 40
GROWS = 120
BF = jnp.bfloat16
F32 = jnp.float32


def top_rows(shape):
    return (lax.broadcasted_iota(jnp.int32, shape, 0) & 7) < 4


def swap_halves(x):
    return pltpu.roll(x, 4, 0)


def fold(x):
    return x + swap_halves(x)


def pieces(x):
    high = x.astype(BF).astype(F32)
    return jnp.where(top_rows(x.shape), high, x - high).astype(BF)


def matmul(a, b):
    return jnp.dot(a, b, preferred_element_type=F32)


def matmul_t(a, b):
    return lax.dot_general(a, b, (((1,), (1,)), ((), ())), preferred_element_type=F32)


def one_hot(ids, rows):
    cell = lax.broadcasted_iota(jnp.int32, (rows, ids.shape[1]), 0)
    return jnp.where(cell == ids, 1.0, 0.0).astype(F32)


def paired(groups):
    out = []
    for j in range(0, len(groups), 2):
        first = groups[j]
        second = groups[min(j + 1, len(groups) - 1)]
        out.append(jnp.where(top_rows(first.shape), first, second))
    return jnp.concatenate(out, axis=0)


def unpaired(x, count):
    out = []
    for g in range(count):
        block = x[(g // 2) * 8 : (g // 2) * 8 + 8]
        turned = swap_halves(block)
        top = top_rows(block.shape)
        out.append(jnp.where(top, block, turned) if g % 2 == 0 else jnp.where(top, turned, block))
    return jnp.concatenate(out, axis=0)


def send_hot(send):
    return jnp.concatenate([one_hot(send[k : k + 1, :], CELLS) for k in range(4)], axis=1).astype(BF)


def write_messages(table, send, parity, near_ref, far_ref):
    listed = matmul(table, send_hot(send))
    groups = [fold(listed[8 * g : 8 * g + 8]) for g in range(listed.shape[0] // 8)]
    packed = paired(groups)
    up, down = packed[:, :128], packed[:, 128:]
    even = parity == 0
    near_ref[...] = jnp.where(even, up, down)
    far_ref[...] = jnp.where(even, down, up)


def ghost_table(near, cross, relay, parity, count):
    rows = near.shape[0]
    first, second = cross[:rows], cross[rows:]
    low = lax.broadcasted_iota(jnp.int32, (rows, 128), 1) < 64
    even = parity == 0
    left = jnp.where(low, jnp.where(even, second, relay), jnp.where(even, first, near))
    right = jnp.where(low, jnp.where(even, near, first), jnp.where(even, relay, second))
    return pieces(unpaired(jnp.concatenate([left, right], axis=1), count))


def send_kernel(parity_ref, state_ref, send_ref, near_ref, far_ref, wide_ref, dense_ref):
    for v in range(NV):
        wide_ref[8 * v : 8 * v + 4, :] = state_ref[v]
        wide_ref[8 * v + 4 : 8 * v + 8, :] = state_ref[v]
    wide = wide_ref[...]
    write_messages(pieces(wide), send_ref[...], parity_ref[0], near_ref, far_ref)
    dense_ref[...] = paired([wide[8 * v : 8 * v + 8] for v in range(NV)])


def gradient_kernel(
    parity_ref, count_ref, wide_ref, near_in, cross_in, relay_in, owner_ref, neighbor_ref, normal_ref,
    volume_ref, send_ref, table_ref, near_ref, far_ref,
):
    parity = parity_ref[0]
    ghosts = ghost_table(near_in[...], cross_in[...], relay_in[...], parity, NV)
    values = jnp.concatenate([pieces(wide_ref[...]), ghosts], axis=1)
    total = jnp.zeros((GROWS, CELLS), F32)
    for f in range(0, FACES, CHUNK):
        own = one_hot(owner_ref[:, f : f + CHUNK], CELLS)
        other = one_hot(neighbor_ref[:, f : f + CHUNK], CELLS + GHOSTS)
        local = other[:CELLS]
        jump_hot = jnp.concatenate([local - own, other[CELLS:]], axis=0).astype(BF)
        sum_hot = (local + own).astype(BF)
        jump = matmul(values, jump_hot)
        jumps = [fold(jump[8 * v : 8 * v + 8]) for v in range(NV)]
        live = lax.broadcasted_iota(jnp.int32, (1, CHUNK), 1) + f < count_ref[0]
        flows = []
        for d in range(3):
            half = jnp.where(live, 0.5 * normal_ref[d : d + 1, f : f + CHUNK], 0.0)
            for v in range(NV):
                flows.append(jumps[v] * half)
        total = total + matmul_t(pieces(jnp.concatenate(flows, axis=0)), sum_hot)
    inverse = 1.0 / volume_ref[...]
    gradient = jnp.concatenate([fold(total[8 * g : 8 * g + 8]) * inverse for g in range(3 * NV)], axis=0)
    table = pieces(gradient)
    table_ref[...] = table
    write_messages(table, send_ref[...], parity, near_ref, far_ref)


def spatial_groups(
    parity_ref, count_ref, wide_ref, near_in, cross_in, relay_in, table_ref, gnear_in, gcross_in, grelay_in,
    owner_ref, neighbor_ref, normal_ref, owner_arm_ref, neighbor_arm_ref, volume_ref,
):
    parity = parity_ref[0]
    ghosts = ghost_table(near_in[...], cross_in[...], relay_in[...], parity, NV)
    grad_ghosts = ghost_table(gnear_in[...], gcross_in[...], grelay_in[...], parity, 3 * NV)
    local = jnp.concatenate([pieces(wide_ref[...]), table_ref[...]], axis=0)
    values = jnp.concatenate([local, jnp.concatenate([ghosts, grad_ghosts], axis=0)], axis=1)
    total = jnp.zeros((VROWS, CELLS), F32)
    top = top_rows((8, CHUNK))
    sign = jnp.where(top, 1.0, -1.0)
    for f in range(0, FACES, CHUNK):
        own = one_hot(owner_ref[:, f : f + CHUNK], CELLS)
        other = one_hot(neighbor_ref[:, f : f + CHUNK], CELLS + GHOSTS)
        difference = (own - other[:CELLS]).astype(BF)
        left = matmul(local, own.astype(BF))
        right = matmul(values, other.astype(BF))
        live = lax.broadcasted_iota(jnp.int32, (1, CHUNK), 1) + f < count_ref[0]
        normals = [jnp.where(live, normal_ref[d : d + 1, f : f + CHUNK], 0.0) for d in range(3)]
        area = jnp.sqrt(normals[0] * normals[0] + normals[1] * normals[1] + normals[2] * normals[2])
        states = []
        for v in range(NV):
            a, b = left[8 * v : 8 * v + 8], right[8 * v : 8 * v + 8]
            for d in range(3):
                g = VROWS + 8 * (NV * d + v)
                a = a + left[g : g + 8] * owner_arm_ref[d : d + 1, f : f + CHUNK]
                b = b + right[g : g + 8] * neighbor_arm_ref[d : d + 1, f : f + CHUNK]
            states.append(jnp.where(top, a, b) + swap_halves(jnp.where(top, b, a)))
        density, energy = states[0], states[4]
        momentum = states[1:4]
        inverse = 1.0 / density
        velocity = [m * inverse for m in momentum]
        kinetic = momentum[0] * velocity[0] + momentum[1] * velocity[1] + momentum[2] * velocity[2]
        pressure = (HEAT_RATIO - 1.0) * (energy - 0.5 * kinetic)
        speed = velocity[0] * normals[0] + velocity[1] * normals[1] + velocity[2] * normals[2]
        wave = jnp.abs(speed) + jnp.sqrt(HEAT_RATIO * pressure * inverse) * area
        wave = jnp.maximum(wave, swap_halves(wave)) * sign
        flux = [density * speed]
        for d in range(3):
            flux.append(momentum[d] * speed + pressure * normals[d])
        flux.append((energy + pressure) * speed)
        faces = [fold(0.5 * (flux[v] + wave * states[v])) for v in range(NV)]
        total = total + matmul_t(pieces(jnp.concatenate(faces, axis=0)), difference)
    inverse = 1.0 / volume_ref[...]
    return [fold(total[8 * v : 8 * v + 8]) * inverse for v in range(NV)]


def middle_kernel(*refs):
    *common, spectral_ref, step_ref, send_ref, wide_out, dense_ref, near_ref, far_ref = refs
    spatial = spatial_groups(*common)
    wide_ref, parity = common[2], common[0][0]
    groups = []
    for v in range(NV):
        rows = slice(8 * v, 8 * v + 8)
        groups.append(wide_ref[rows] - 0.5 * step_ref[...] * (spatial[v] + spectral_ref[rows]))
    wide = jnp.concatenate(groups, axis=0)
    wide_out[...] = wide
    dense_ref[...] = paired(groups)
    write_messages(pieces(wide), send_ref[...], parity, near_ref, far_ref)


def last_kernel(*refs):
    *common, spectral_ref, step_ref, state_ref, new_ref, residual_ref = refs
    spatial = spatial_groups(*common)
    for v in range(NV):
        rate = (spatial[v] + spectral_ref[8 * v : 8 * v + 8])[:4]
        residual_ref[v] = rate
        new_ref[v] = state_ref[v] - step_ref[...] * rate


def spectral_kernel(index_ref, matrix_ref, mine_ref, next_ref, rest_ref, out_ref):
    matrix = matrix_ref[index_ref[0]]
    data = jnp.concatenate([mine_ref[...], next_ref[...], rest_ref[...]], axis=0)
    m_high, d_high = matrix.astype(BF), data.astype(BF)
    m_low, d_low = (matrix - m_high.astype(F32)).astype(BF), (data - d_high.astype(F32)).astype(BF)
    out_ref[...] = matmul(m_high, d_high) + matmul(m_high, d_low) + matmul(m_low, d_high)


def spectral_matrices(groups, size):
    points = groups * size
    distance = np.arange(points)[:, None] - np.arange(points)[None, :]
    safe = np.where(distance == 0, 1, distance)
    table = 0.5 * np.where(distance % 2 == 0, 1.0, -1.0) / np.tan(np.pi * safe / points)
    table = np.where(distance == 0, 0.0, table) * FREQUENCY
    out = np.zeros((groups, VROWS, groups * 24), np.float32)
    for y in range(groups):
        for v in range(NV):
            for s in range(8):
                for b in range(groups):
                    for t in range(size):
                        column = b * 24 + (v // 2) * 8 + (v % 2) * 4 + t
                        out[y, 8 * v + s, column] = table[size * y + s % size, size * (y ^ (0, 2, 1, 3)[b]) + t]
    return out


def call(kernel, outputs, scalars, arrays):
    smem = pl.BlockSpec(memory_space=pltpu.SMEM)
    vmem = pl.BlockSpec(memory_space=pltpu.VMEM)
    return pl.pallas_call(
        kernel,
        out_shape=[jax.ShapeDtypeStruct(s, d) for s, d in outputs],
        in_specs=[smem] * len(scalars) + [vmem] * len(arrays),
        out_specs=[vmem] * len(outputs),
        compiler_params=pltpu.CompilerParams(vmem_limit_bytes=32 << 20),
    )(*scalars, *arrays)


def local(
    state, cell_volume, step_size, face_normal, owner_arm, neighbor_arm, face_owner, face_neighbor, face_count,
    send_cells,
):
    parts = lax.axis_size("dom")
    place = lax.axis_index("dom")
    parity = (place & 1).astype(jnp.int32).reshape(1)
    line = lax.axis_index("inst").astype(jnp.int32).reshape(1)
    volume = cell_volume.reshape(1, CELLS)
    step = step_size.reshape(1, CELLS)
    owner = face_owner.reshape(1, FACES)
    neighbor = face_neighbor.reshape(1, FACES)
    matrices = jnp.asarray(spectral_matrices(lax.axis_size("inst"), state.shape[1]))
    inside = [(i, i ^ 1) for i in range(parts)]
    across = [(i, (i + 1) % parts) for i in range(1, parts, 2)] + [((i + 1) % parts, i) for i in range(1, parts, 2)]

    def exchange(near, far):
        got = lax.ppermute(near, "dom", inside)
        outgoing = jnp.concatenate([far, got], axis=0)
        cross = lax.ppermute(outgoing, "dom", across)
        relay = lax.ppermute(cross[: far.shape[0]], "dom", inside)
        return got, cross, relay

    def instances(dense):
        one = lax.ppermute(dense, "inst", [(i, i ^ 2) for i in range(4)])
        outgoing = jnp.concatenate([dense, one], axis=0)
        two = lax.ppermute(outgoing, "inst", [(i, i ^ 1) for i in range(4)])
        return call(spectral_kernel, [((VROWS, CELLS), F32)], [line], [matrices, dense, one, two])[0]

    def message(rows):
        return [((rows, 128), F32)] * 2

    wide_shape, dense_shape = ((VROWS, CELLS), F32), ((24, CELLS), F32)
    geometry = [owner, neighbor, face_normal]
    arms = [owner_arm, neighbor_arm, volume]
    near, far, wide, dense = call(send_kernel, message(24) + [wide_shape, dense_shape], [parity], [state, send_cells])
    for section in range(2):
        ghosts = exchange(near, far)
        spectral = instances(dense)
        table, gnear, gfar = call(
            gradient_kernel, [((GROWS, CELLS), BF)] + message(64), [parity, face_count],
            [wide, *ghosts, *geometry, volume, send_cells],
        )
        gradient_ghosts = exchange(gnear, gfar)
        common = [wide, *ghosts, table, *gradient_ghosts, *geometry, *arms, spectral, step]
        if section == 0:
            wide, dense, near, far = call(
                middle_kernel, [wide_shape, dense_shape] + message(24), [parity, face_count], [*common, send_cells],
            )
    shape = state.shape
    return tuple(call(last_kernel, [(shape, F32)] * 2, [parity, face_count], [*common, state]))


def solution(mesh):
    placed = (
        P(None, "inst", "dom"), P("dom"), P("dom"), P(None, "dom"), P(None, "dom"), P(None, "dom"), P("dom"), P("dom"),
        P("dom"), P("dom", None),
    )
    return jax.shard_map(
        local, mesh=mesh, in_specs=placed, out_specs=(P(None, "inst", "dom"), P(None, "inst", "dom")), check_vma=False,
    )
```

```python
import jax
import jax.numpy as jnp
import numpy as np
from jax import lax
from jax.experimental import pallas as pl
from jax.experimental.pallas import tpu as pltpu
from jax.sharding import PartitionSpec as P


HEAT_RATIO = 1.4
FREQUENCY = 0.5
NV = 5
CELLS = 512
GHOSTS = 256
FACES = 2048
CHUNK = 512
VROWS = 40
GROWS = 120
BF = jnp.bfloat16
F32 = jnp.float32


def parity_of_partition():
    return lax.axis_index("dom") & 1


def top_rows(shape):
    return (lax.broadcasted_iota(jnp.int32, shape, 0) & 7) < 4


def swap_halves(x):
    return pltpu.roll(x, 4, 0)


def fold(x):
    return x + swap_halves(x)


def pieces(x):
    high = x.astype(BF).astype(F32)
    return jnp.where(top_rows(x.shape), high, x - high).astype(BF)


def matmul(a, b):
    return jnp.dot(a, b, preferred_element_type=F32)


def matmul_t(a, b):
    return lax.dot_general(a, b, (((1,), (1,)), ((), ())), preferred_element_type=F32)


def one_hot(ids, rows):
    cell = lax.broadcasted_iota(jnp.int32, (rows, ids.shape[1]), 0)
    return jnp.where(cell == ids, 1.0, 0.0)


def paired(groups):
    out = []
    for j in range(0, len(groups), 2):
        first = groups[j]
        second = groups[min(j + 1, len(groups) - 1)]
        out.append(jnp.where(top_rows(first.shape), first, second))
    return jnp.concatenate(out, axis=0)


def unpaired(x, count):
    out = []
    for g in range(count):
        block = x[(g // 2) * 8 : (g // 2) * 8 + 8]
        turned = swap_halves(block)
        top = top_rows(block.shape)
        out.append(jnp.where(top, block, turned) if g % 2 == 0 else jnp.where(top, turned, block))
    return jnp.concatenate(out, axis=0)


def send_hot(send):
    return jnp.concatenate([one_hot(send[k : k + 1, :], CELLS) for k in range(4)], axis=1).astype(BF)


def write_messages(table, send, parity, near_ref, far_ref):
    listed = matmul(table, send_hot(send))
    groups = [fold(listed[8 * g : 8 * g + 8]) for g in range(listed.shape[0] // 8)]
    packed = paired(groups)
    up, down = packed[:, :128], packed[:, 128:]
    even = parity == 0
    near_ref[...] = jnp.where(even, up, down)
    far_ref[...] = jnp.where(even, down, up)


def ghost_table(near, cross, relay, parity, count):
    rows = near.shape[0]
    first, second = cross[:rows], cross[rows:]
    low = lax.broadcasted_iota(jnp.int32, (rows, 128), 1) < 64
    even = parity == 0
    left = jnp.where(low, jnp.where(even, second, relay), jnp.where(even, first, near))
    right = jnp.where(low, jnp.where(even, near, first), jnp.where(even, relay, second))
    return pieces(unpaired(jnp.concatenate([left, right], axis=1), count))


def send_kernel(
    state_hbm, send_hbm, near_ref, far_ref, wide_ref, dense_ref, state_ref, send_ref, state_sem, send_sem
):
    fetch_state = pltpu.make_async_copy(state_hbm, state_ref, state_sem)
    fetch_send = pltpu.make_async_copy(send_hbm, send_ref, send_sem)
    fetch_state.start()
    fetch_send.start()
    fetch_send.wait()
    fetch_state.wait()
    for v in range(NV):
        wide_ref[8 * v : 8 * v + 4, :] = state_ref[v]
        wide_ref[8 * v + 4 : 8 * v + 8, :] = state_ref[v]
    wide = wide_ref[...]
    write_messages(pieces(wide), send_ref[...], parity_of_partition(), near_ref, far_ref)
    dense_ref[...] = paired([wide[8 * v : 8 * v + 8] for v in range(NV)])


def hot_kernel(owner_ref, neighbor_ref, own_ref, other_ref):
    for f in range(0, FACES, CHUNK):
        faces = slice(f, f + CHUNK)
        own_ref[:, faces] = one_hot(owner_ref[:, faces], CELLS).astype(BF)
        other_ref[:, faces] = one_hot(neighbor_ref[:, faces], CELLS + GHOSTS).astype(BF)


def jump_kernel(wide_ref, own_ref, other_ref, jump_ref):
    values = pieces(wide_ref[...])
    for f in range(0, FACES, CHUNK):
        faces = slice(f, f + CHUNK)
        jump_ref[:, faces] = matmul(values, other_ref[:CELLS, faces] - own_ref[:, faces])


def gradient_kernel(
    count_ref, jump_ref, near_in, cross_in, relay_in, own_ref, other_ref, normal_ref, volume_ref, send_ref,
    table_ref, near_ref, far_ref,
):
    parity = parity_of_partition()
    ghosts = ghost_table(near_in[...], cross_in[...], relay_in[...], parity, NV)
    total = jnp.zeros((GROWS, CELLS), F32)
    for f in range(0, FACES, CHUNK):
        faces = slice(f, f + CHUNK)
        jump = jump_ref[:, faces] + matmul(ghosts, other_ref[CELLS:, faces])
        jumps = [fold(jump[8 * v : 8 * v + 8]) for v in range(NV)]
        live = lax.broadcasted_iota(jnp.int32, (1, CHUNK), 1) + f < count_ref[0]
        flows = []
        for d in range(3):
            half = jnp.where(live, 0.5 * normal_ref[d : d + 1, faces], 0.0)
            for v in range(NV):
                flows.append(jumps[v] * half)
        sum_hot = other_ref[:CELLS, faces] + own_ref[:, faces]
        total = total + matmul_t(pieces(jnp.concatenate(flows, axis=0)), sum_hot)
    inverse = 1.0 / volume_ref[...]
    gradient = jnp.concatenate([fold(total[8 * g : 8 * g + 8]) * inverse for g in range(3 * NV)], axis=0)
    table = pieces(gradient)
    table_ref[...] = table
    write_messages(table, send_ref[...], parity, near_ref, far_ref)


def with_arms(values, arm_ref, faces):
    arms = [arm_ref[d : d + 1, faces] for d in range(3)]
    out = []
    for v in range(NV):
        total = values[8 * v : 8 * v + 8]
        for d in range(3):
            g = VROWS + 8 * (NV * d + v)
            total = total + values[g : g + 8] * arms[d]
        out.append(total)
    return out


def face_kernel(wide_ref, table_ref, own_ref, other_ref, owner_arm_ref, neighbor_arm_ref, face_ref):
    values = jnp.concatenate([pieces(wide_ref[...]), table_ref[...]], axis=0)
    top = top_rows((8, CHUNK))
    for f in range(0, FACES, CHUNK):
        faces = slice(f, f + CHUNK)
        left = with_arms(matmul(values, own_ref[:, faces]), owner_arm_ref, faces)
        right = with_arms(matmul(values, other_ref[:CELLS, faces]), neighbor_arm_ref, faces)
        for v in range(NV):
            a, b = left[v], right[v]
            face_ref[8 * v : 8 * v + 8, faces] = jnp.where(top, a, b) + swap_halves(jnp.where(top, b, a))


def spatial_groups(
    count_ref, face_ref, near_in, cross_in, relay_in, gnear_in, gcross_in, grelay_in, own_ref, other_ref,
    normal_ref, neighbor_arm_ref, volume_ref,
):
    parity = parity_of_partition()
    ghosts = ghost_table(near_in[...], cross_in[...], relay_in[...], parity, NV)
    grad_ghosts = ghost_table(gnear_in[...], gcross_in[...], grelay_in[...], parity, 3 * NV)
    values = jnp.concatenate([ghosts, grad_ghosts], axis=0)
    total = jnp.zeros((VROWS, CELLS), F32)
    top = top_rows((8, CHUNK))
    sign = jnp.where(top, 1.0, -1.0)
    for f in range(0, FACES, CHUNK):
        faces = slice(f, f + CHUNK)
        right = with_arms(matmul(values, other_ref[CELLS:, faces]), neighbor_arm_ref, faces)
        live = lax.broadcasted_iota(jnp.int32, (1, CHUNK), 1) + f < count_ref[0]
        normals = [jnp.where(live, normal_ref[d : d + 1, faces], 0.0) for d in range(3)]
        area = jnp.sqrt(normals[0] * normals[0] + normals[1] * normals[1] + normals[2] * normals[2])
        states = [face_ref[8 * v : 8 * v + 8, faces] + jnp.where(top, 0.0, fold(right[v])) for v in range(NV)]
        density, energy = states[0], states[4]
        momentum = states[1:4]
        inverse = 1.0 / density
        velocity = [m * inverse for m in momentum]
        kinetic = momentum[0] * velocity[0] + momentum[1] * velocity[1] + momentum[2] * velocity[2]
        pressure = (HEAT_RATIO - 1.0) * (energy - 0.5 * kinetic)
        speed = velocity[0] * normals[0] + velocity[1] * normals[1] + velocity[2] * normals[2]
        wave = jnp.abs(speed) + jnp.sqrt(HEAT_RATIO * pressure * inverse) * area
        wave = jnp.maximum(wave, swap_halves(wave)) * sign
        flux = [density * speed]
        for d in range(3):
            flux.append(momentum[d] * speed + pressure * normals[d])
        flux.append((energy + pressure) * speed)
        fluxes = [fold(0.5 * (flux[v] + wave * states[v])) for v in range(NV)]
        difference = own_ref[:, faces] - other_ref[:CELLS, faces]
        total = total + matmul_t(pieces(jnp.concatenate(fluxes, axis=0)), difference)
    inverse = 1.0 / volume_ref[...]
    return [fold(total[8 * v : 8 * v + 8]) * inverse for v in range(NV)]


def middle_kernel(*refs):
    *common, spectral_ref, step_ref, wide_ref, send_ref, wide_out, dense_ref, near_ref, far_ref = refs
    spatial = spatial_groups(*common)
    groups = []
    for v in range(NV):
        rows = slice(8 * v, 8 * v + 8)
        groups.append(wide_ref[rows] - 0.5 * step_ref[...] * (spatial[v] + spectral_ref[rows]))
    wide = jnp.concatenate(groups, axis=0)
    wide_out[...] = wide
    dense_ref[...] = paired(groups)
    write_messages(pieces(wide), send_ref[...], parity_of_partition(), near_ref, far_ref)


def last_kernel(*refs):
    *common, spectral_ref, step_ref, state_ref, new_ref, residual_ref = refs
    spatial = spatial_groups(*common)
    for v in range(NV):
        rate = (spatial[v] + spectral_ref[8 * v : 8 * v + 8])[:4]
        residual_ref[v] = rate
        new_ref[v] = state_ref[v] - step_ref[...] * rate


def spectral_kernel(matrix_ref, mine_ref, next_ref, rest_ref, out_ref):
    matrix = matrix_ref[lax.axis_index("inst")]
    data = jnp.concatenate([mine_ref[...], next_ref[...], rest_ref[...]], axis=0)
    m_high, d_high = matrix.astype(BF), data.astype(BF)
    m_low, d_low = (matrix - m_high.astype(F32)).astype(BF), (data - d_high.astype(F32)).astype(BF)
    out_ref[...] = matmul(m_high, d_high) + matmul(m_high, d_low) + matmul(m_low, d_high)


def spectral_matrices(groups, size):
    points = groups * size
    distance = np.arange(points)[:, None] - np.arange(points)[None, :]
    safe = np.where(distance == 0, 1, distance)
    table = 0.5 * np.where(distance % 2 == 0, 1.0, -1.0) / np.tan(np.pi * safe / points)
    table = np.where(distance == 0, 0.0, table) * FREQUENCY
    out = np.zeros((groups, VROWS, groups * 24), np.float32)
    for y in range(groups):
        for v in range(NV):
            for s in range(8):
                for b in range(groups):
                    for t in range(size):
                        column = b * 24 + (v // 2) * 8 + (v % 2) * 4 + t
                        out[y, 8 * v + s, column] = table[size * y + s % size, size * (y ^ (0, 1, 3, 2)[b]) + t]
    return out


def call(kernel, outputs, scalars, arrays, hbm=0, scratch=(), limit=8):
    smem = pl.BlockSpec(memory_space=pltpu.SMEM)
    vmem = pl.BlockSpec(memory_space=pltpu.VMEM)
    far = pl.BlockSpec(memory_space=pltpu.HBM)
    return pl.pallas_call(
        kernel,
        out_shape=[jax.ShapeDtypeStruct(s, d) for s, d in outputs],
        in_specs=[smem] * len(scalars) + [far] * hbm + [vmem] * (len(arrays) - hbm),
        out_specs=[vmem] * len(outputs),
        scratch_shapes=scratch,
        compiler_params=pltpu.CompilerParams(vmem_limit_bytes=limit << 20),
    )(*scalars, *arrays)


def local(
    state, cell_volume, step_size, face_normal, owner_arm, neighbor_arm, face_owner, face_neighbor, face_count,
    send_cells,
):
    parts = lax.axis_size("dom")
    volume = cell_volume.reshape(1, CELLS)
    step = step_size.reshape(1, CELLS)
    owner = face_owner.reshape(1, FACES)
    neighbor = face_neighbor.reshape(1, FACES)
    matrices = jnp.asarray(spectral_matrices(lax.axis_size("inst"), state.shape[1]))
    inside = [(i, i ^ 1) for i in range(parts)]
    across = [(i, (i + 1) % parts) for i in range(1, parts, 2)] + [((i + 1) % parts, i) for i in range(1, parts, 2)]

    def exchange(near, far):
        got = lax.ppermute(near, "dom", inside)
        outgoing = jnp.concatenate([far, got], axis=0)
        cross = lax.ppermute(outgoing, "dom", across)
        relay = lax.ppermute(cross[: far.shape[0]], "dom", inside)
        return got, cross, relay

    def instances(dense):
        one = lax.ppermute(dense, "inst", [(i, i ^ 1) for i in range(4)])
        outgoing = jnp.concatenate([dense, one], axis=0)
        rest = lax.ppermute(outgoing, "inst", [(i, i ^ 3) for i in range(4)])
        arrays = [matrices, dense, one, rest]
        return call(spectral_kernel, [((VROWS, CELLS), F32)], [], arrays)[0]

    def message(rows):
        return [((rows, 128), F32)] * 2

    wide_shape, dense_shape = ((VROWS, CELLS), F32), ((24, CELLS), F32)
    faces_shape = ((VROWS, FACES), F32)
    near, far, wide, dense = call(
        send_kernel, message(24) + [wide_shape, dense_shape], [], [state, send_cells], hbm=2,
        scratch=[
            pltpu.VMEM(state.shape, F32), pltpu.VMEM(send_cells.shape, jnp.int32), pltpu.SemaphoreType.DMA,
            pltpu.SemaphoreType.DMA,
        ],
    )
    hot = call(hot_kernel, [((CELLS, FACES), BF), ((CELLS + GHOSTS, FACES), BF)], [], [owner, neighbor])
    for section in range(2):
        jump = call(jump_kernel, [faces_shape], [], [wide, *hot])[0]
        ghosts = exchange(near, far)
        spectral = instances(dense)
        table, gnear, gfar = call(
            gradient_kernel, [((GROWS, CELLS), BF)] + message(64), [face_count],
            [jump, *ghosts, *hot, face_normal, volume, send_cells],
        )
        face = call(face_kernel, [faces_shape], [], [wide, table, *hot, owner_arm, neighbor_arm])[0]
        gradient_ghosts = exchange(gnear, gfar)
        common = [face, *ghosts, *gradient_ghosts, *hot, face_normal, neighbor_arm, volume, spectral, step]
        if section == 0:
            wide, dense, near, far = call(
                middle_kernel, [wide_shape, dense_shape] + message(24), [face_count],
                [*common, wide, send_cells],
            )
    return tuple(call(last_kernel, [(state.shape, F32)] * 2, [face_count], [*common, state]))


def solution(mesh):
    placed = (
        P(None, "inst", "dom"), P("dom"), P("dom"), P(None, "dom"), P(None, "dom"), P(None, "dom"), P("dom"), P("dom"),
        P("dom"), P("dom", None),
    )
    return jax.shard_map(
        local, mesh=mesh, in_specs=placed, out_specs=(P(None, "inst", "dom"), P(None, "inst", "dom")), check_vma=False,
    )
```

```python
import jax
import jax.numpy as jnp
import numpy as np
from jax import lax
from jax.experimental import pallas as pl
from jax.experimental.pallas import tpu as pltpu
from jax.sharding import PartitionSpec as P


HEAT_RATIO = 1.4
FREQUENCY = 0.5
NV = 5
CELLS = 512
GHOSTS = 256
FACES = 2048
CHUNK = 512
VROWS = 40
GROWS = 120
BF = jnp.bfloat16
F32 = jnp.float32


def parity_of_partition():
    return lax.axis_index("dom") & 1


def top_rows(shape):
    return (lax.broadcasted_iota(jnp.int32, shape, 0) & 7) < 4


def swap_halves(x):
    return pltpu.roll(x, 4, 0)


def fold(x):
    return x + swap_halves(x)


def pieces(x):
    high = x.astype(BF).astype(F32)
    return jnp.where(top_rows(x.shape), high, x - high).astype(BF)


def matmul(a, b):
    return jnp.dot(a, b, preferred_element_type=F32)


def matmul_t(a, b):
    return lax.dot_general(a, b, (((1,), (1,)), ((), ())), preferred_element_type=F32)


def one_hot(ids, rows):
    cell = lax.broadcasted_iota(jnp.int32, (rows, ids.shape[1]), 0)
    return jnp.where(cell == ids, 1.0, 0.0)


def paired(groups):
    out = []
    for j in range(0, len(groups), 2):
        first = groups[j]
        second = groups[min(j + 1, len(groups) - 1)]
        out.append(jnp.where(top_rows(first.shape), first, second))
    return jnp.concatenate(out, axis=0)


def unpaired(x, count):
    out = []
    for g in range(count):
        block = x[(g // 2) * 8 : (g // 2) * 8 + 8]
        turned = swap_halves(block)
        top = top_rows(block.shape)
        out.append(jnp.where(top, block, turned) if g % 2 == 0 else jnp.where(top, turned, block))
    return jnp.concatenate(out, axis=0)


def send_hot(send):
    return jnp.concatenate([one_hot(send[k : k + 1, :], CELLS) for k in range(4)], axis=1).astype(BF)


def write_messages(table, send, parity, near_ref, far_ref):
    listed = matmul(table, send_hot(send))
    groups = [fold(listed[8 * g : 8 * g + 8]) for g in range(listed.shape[0] // 8)]
    packed = paired(groups)
    up, down = packed[:, :128], packed[:, 128:]
    even = parity == 0
    near_ref[...] = jnp.where(even, up, down)
    far_ref[...] = jnp.where(even, down, up)


def ghost_table(near, cross, relay, parity, count):
    rows = near.shape[0]
    first, second = cross[:rows], cross[rows:]
    low = lax.broadcasted_iota(jnp.int32, (rows, 128), 1) < 64
    even = parity == 0
    left = jnp.where(low, jnp.where(even, second, relay), jnp.where(even, first, near))
    right = jnp.where(low, jnp.where(even, near, first), jnp.where(even, relay, second))
    return pieces(unpaired(jnp.concatenate([left, right], axis=1), count))


def send_kernel(
    state_hbm, send_hbm, owner_hbm, neighbor_hbm, near_ref, far_ref, wide_ref, dense_ref, owner_ref, neighbor_ref,
    state_ref, send_ref, state_sem, send_sem, owner_sem, neighbor_sem,
):
    fetch_send = pltpu.make_async_copy(send_hbm, send_ref, send_sem)
    fetch_state = pltpu.make_async_copy(state_hbm, state_ref, state_sem)
    fetch_owner = pltpu.make_async_copy(owner_hbm, owner_ref, owner_sem)
    fetch_neighbor = pltpu.make_async_copy(neighbor_hbm, neighbor_ref, neighbor_sem)
    for fetch in (fetch_send, fetch_state, fetch_owner, fetch_neighbor):
        fetch.start()
    fetch_send.wait()
    fetch_state.wait()
    for v in range(NV):
        wide_ref[8 * v : 8 * v + 4, :] = state_ref[v]
        wide_ref[8 * v + 4 : 8 * v + 8, :] = state_ref[v]
    wide = wide_ref[...]
    write_messages(pieces(wide), send_ref[...], parity_of_partition(), near_ref, far_ref)
    dense_ref[...] = paired([wide[8 * v : 8 * v + 8] for v in range(NV)])
    fetch_owner.wait()
    fetch_neighbor.wait()


def hot_kernel(owner_ref, neighbor_ref, own_ref, other_ref):
    for f in range(0, FACES, CHUNK):
        faces = slice(f, f + CHUNK)
        own_ref[:, faces] = one_hot(owner_ref[:, faces], CELLS).astype(BF)
        other_ref[:, faces] = one_hot(neighbor_ref[:, faces], CELLS + GHOSTS).astype(BF)


def jump_kernel(wide_ref, own_ref, other_ref, jump_ref):
    values = pieces(wide_ref[...])
    for f in range(0, FACES, CHUNK):
        faces = slice(f, f + CHUNK)
        jump_ref[:, faces] = matmul(values, other_ref[:CELLS, faces] - own_ref[:, faces])


def gradient_kernel(
    count_ref, jump_ref, near_in, cross_in, relay_in, own_ref, other_ref, normal_ref, volume_ref, send_ref,
    table_ref, near_ref, far_ref,
):
    parity = parity_of_partition()
    ghosts = ghost_table(near_in[...], cross_in[...], relay_in[...], parity, NV)
    total = jnp.zeros((GROWS, CELLS), F32)
    for f in range(0, FACES, CHUNK):
        faces = slice(f, f + CHUNK)
        jump = jump_ref[:, faces] + matmul(ghosts, other_ref[CELLS:, faces])
        jumps = [fold(jump[8 * v : 8 * v + 8]) for v in range(NV)]
        live = lax.broadcasted_iota(jnp.int32, (1, CHUNK), 1) + f < count_ref[0]
        flows = []
        for d in range(3):
            half = jnp.where(live, 0.5 * normal_ref[d : d + 1, faces], 0.0)
            for v in range(NV):
                flows.append(jumps[v] * half)
        sum_hot = other_ref[:CELLS, faces] + own_ref[:, faces]
        total = total + matmul_t(pieces(jnp.concatenate(flows, axis=0)), sum_hot)
    inverse = 1.0 / volume_ref[...]
    gradient = jnp.concatenate([fold(total[8 * g : 8 * g + 8]) * inverse for g in range(3 * NV)], axis=0)
    table = pieces(gradient)
    table_ref[...] = table
    write_messages(table, send_ref[...], parity, near_ref, far_ref)


def with_arms(values, arm_ref, faces):
    arms = [arm_ref[d : d + 1, faces] for d in range(3)]
    out = []
    for v in range(NV):
        total = values[8 * v : 8 * v + 8]
        for d in range(3):
            g = VROWS + 8 * (NV * d + v)
            total = total + values[g : g + 8] * arms[d]
        out.append(total)
    return out


def face_kernel(wide_ref, table_ref, own_ref, other_ref, owner_arm_ref, neighbor_arm_ref, face_ref):
    values = jnp.concatenate([pieces(wide_ref[...]), table_ref[...]], axis=0)
    top = top_rows((8, CHUNK))
    for f in range(0, FACES, CHUNK):
        faces = slice(f, f + CHUNK)
        left = with_arms(matmul(values, own_ref[:, faces]), owner_arm_ref, faces)
        right = with_arms(matmul(values, other_ref[:CELLS, faces]), neighbor_arm_ref, faces)
        for v in range(NV):
            a, b = left[v], right[v]
            face_ref[8 * v : 8 * v + 8, faces] = jnp.where(top, a, b) + swap_halves(jnp.where(top, b, a))


def spatial_groups(
    count_ref, face_ref, near_in, cross_in, relay_in, gnear_in, gcross_in, grelay_in, own_ref, other_ref,
    normal_ref, neighbor_arm_ref, volume_ref,
):
    parity = parity_of_partition()
    ghosts = ghost_table(near_in[...], cross_in[...], relay_in[...], parity, NV)
    grad_ghosts = ghost_table(gnear_in[...], gcross_in[...], grelay_in[...], parity, 3 * NV)
    values = jnp.concatenate([ghosts, grad_ghosts], axis=0)
    total = jnp.zeros((VROWS, CELLS), F32)
    top = top_rows((8, CHUNK))
    sign = jnp.where(top, 1.0, -1.0)
    for f in range(0, FACES, CHUNK):
        faces = slice(f, f + CHUNK)
        right = with_arms(matmul(values, other_ref[CELLS:, faces]), neighbor_arm_ref, faces)
        live = lax.broadcasted_iota(jnp.int32, (1, CHUNK), 1) + f < count_ref[0]
        normals = [jnp.where(live, normal_ref[d : d + 1, faces], 0.0) for d in range(3)]
        area = jnp.sqrt(normals[0] * normals[0] + normals[1] * normals[1] + normals[2] * normals[2])
        states = [face_ref[8 * v : 8 * v + 8, faces] + jnp.where(top, 0.0, fold(right[v])) for v in range(NV)]
        density, energy = states[0], states[4]
        momentum = states[1:4]
        inverse = 1.0 / density
        velocity = [m * inverse for m in momentum]
        kinetic = momentum[0] * velocity[0] + momentum[1] * velocity[1] + momentum[2] * velocity[2]
        pressure = (HEAT_RATIO - 1.0) * (energy - 0.5 * kinetic)
        speed = velocity[0] * normals[0] + velocity[1] * normals[1] + velocity[2] * normals[2]
        wave = jnp.abs(speed) + jnp.sqrt(HEAT_RATIO * pressure * inverse) * area
        wave = jnp.maximum(wave, swap_halves(wave)) * sign
        flux = [density * speed]
        for d in range(3):
            flux.append(momentum[d] * speed + pressure * normals[d])
        flux.append((energy + pressure) * speed)
        fluxes = [fold(0.5 * (flux[v] + wave * states[v])) for v in range(NV)]
        difference = own_ref[:, faces] - other_ref[:CELLS, faces]
        total = total + matmul_t(pieces(jnp.concatenate(fluxes, axis=0)), difference)
    inverse = 1.0 / volume_ref[...]
    return [fold(total[8 * v : 8 * v + 8]) * inverse for v in range(NV)]


def middle_kernel(*refs):
    *common, spectral_ref, step_ref, wide_ref, send_ref, wide_out, dense_ref, near_ref, far_ref = refs
    spatial = spatial_groups(*common)
    groups = []
    for v in range(NV):
        rows = slice(8 * v, 8 * v + 8)
        groups.append(wide_ref[rows] - 0.5 * step_ref[...] * (spatial[v] + spectral_ref[rows]))
    wide = jnp.concatenate(groups, axis=0)
    wide_out[...] = wide
    dense_ref[...] = paired(groups)
    write_messages(pieces(wide), send_ref[...], parity_of_partition(), near_ref, far_ref)


def last_kernel(*refs):
    *common, spectral_ref, step_ref, state_ref, new_ref, residual_ref = refs
    spatial = spatial_groups(*common)
    for v in range(NV):
        rate = (spatial[v] + spectral_ref[8 * v : 8 * v + 8])[:4]
        residual_ref[v] = rate
        new_ref[v] = state_ref[v] - step_ref[...] * rate


def spectral_kernel(matrix_ref, mine_ref, next_ref, rest_ref, out_ref):
    matrix = matrix_ref[lax.axis_index("inst")]
    data = jnp.concatenate([mine_ref[...], next_ref[...], rest_ref[...]], axis=0)
    m_high, d_high = matrix.astype(BF), data.astype(BF)
    m_low, d_low = (matrix - m_high.astype(F32)).astype(BF), (data - d_high.astype(F32)).astype(BF)
    out_ref[...] = matmul(m_high, d_high) + matmul(m_high, d_low) + matmul(m_low, d_high)


def spectral_matrices(groups, size):
    points = groups * size
    distance = np.arange(points)[:, None] - np.arange(points)[None, :]
    safe = np.where(distance == 0, 1, distance)
    table = 0.5 * np.where(distance % 2 == 0, 1.0, -1.0) / np.tan(np.pi * safe / points)
    table = np.where(distance == 0, 0.0, table) * FREQUENCY
    out = np.zeros((groups, VROWS, groups * 24), np.float32)
    for y in range(groups):
        for v in range(NV):
            for s in range(8):
                for b in range(groups):
                    for t in range(size):
                        column = b * 24 + (v // 2) * 8 + (v % 2) * 4 + t
                        out[y, 8 * v + s, column] = table[size * y + s % size, size * (y ^ (0, 1, 3, 2)[b]) + t]
    return out


def call(kernel, outputs, scalars, arrays, hbm=0, scratch=(), limit=8):
    smem = pl.BlockSpec(memory_space=pltpu.SMEM)
    vmem = pl.BlockSpec(memory_space=pltpu.VMEM)
    far = pl.BlockSpec(memory_space=pltpu.HBM)
    return pl.pallas_call(
        kernel,
        out_shape=[jax.ShapeDtypeStruct(s, d) for s, d in outputs],
        in_specs=[smem] * len(scalars) + [far] * hbm + [vmem] * (len(arrays) - hbm),
        out_specs=[vmem] * len(outputs),
        scratch_shapes=scratch,
        compiler_params=pltpu.CompilerParams(vmem_limit_bytes=limit << 20),
    )(*scalars, *arrays)


def local(
    state, cell_volume, step_size, face_normal, owner_arm, neighbor_arm, face_owner, face_neighbor, face_count,
    send_cells,
):
    parts = lax.axis_size("dom")
    volume = cell_volume.reshape(1, CELLS)
    step = step_size.reshape(1, CELLS)
    owner = face_owner.reshape(1, FACES)
    neighbor = face_neighbor.reshape(1, FACES)
    matrices = jnp.asarray(spectral_matrices(lax.axis_size("inst"), state.shape[1]))
    inside = [(i, i ^ 1) for i in range(parts)]
    lines = lax.axis_size("inst")
    across = []
    for i in range(parts):
        for y in range(lines):
            j = i + 1 if i % 2 else i - 1
            across.append((lines * i + y, lines * j + y if 0 <= j < parts else lines * i + (y ^ 1)))

    def exchange(near, far):
        got = lax.ppermute(near, "dom", inside)
        outgoing = jnp.concatenate([far, got], axis=0)
        cross = lax.ppermute(outgoing, ("dom", "inst"), across)
        relay = lax.ppermute(cross[: far.shape[0]], "dom", inside)
        return got, cross, relay

    def instances(dense):
        one = lax.ppermute(dense, "inst", [(i, i ^ 1) for i in range(4)])
        outgoing = jnp.concatenate([dense, one], axis=0)
        rest = lax.ppermute(outgoing, "inst", [(i, i ^ 3) for i in range(4)])
        arrays = [matrices, dense, one, rest]
        return call(spectral_kernel, [((VROWS, CELLS), F32)], [], arrays)[0]

    def message(rows):
        return [((rows, 128), F32)] * 2

    wide_shape, dense_shape = ((VROWS, CELLS), F32), ((24, CELLS), F32)
    faces_shape = ((VROWS, FACES), F32)
    sources = [pltpu.with_memory_space_constraint(x, pltpu.HBM) for x in (state, send_cells, owner, neighbor)]
    ids = ((1, FACES), jnp.int32)
    near, far, wide, dense, owner, neighbor = call(
        send_kernel, message(24) + [wide_shape, dense_shape, ids, ids], [], sources, hbm=4,
        scratch=[pltpu.VMEM(state.shape, F32), pltpu.VMEM(send_cells.shape, jnp.int32)] + [pltpu.SemaphoreType.DMA] * 4,
    )
    hot = call(hot_kernel, [((CELLS, FACES), BF), ((CELLS + GHOSTS, FACES), BF)], [], [owner, neighbor])
    for section in range(2):
        jump = call(jump_kernel, [faces_shape], [], [wide, *hot])[0]
        ghosts = exchange(near, far)
        spectral = instances(dense)
        table, gnear, gfar = call(
            gradient_kernel, [((GROWS, CELLS), BF)] + message(64), [face_count],
            [jump, *ghosts, *hot, face_normal, volume, send_cells],
        )
        face = call(face_kernel, [faces_shape], [], [wide, table, *hot, owner_arm, neighbor_arm])[0]
        gradient_ghosts = exchange(gnear, gfar)
        common = [face, *ghosts, *gradient_ghosts, *hot, face_normal, neighbor_arm, volume, spectral, step]
        if section == 0:
            wide, dense, near, far = call(
                middle_kernel, [wide_shape, dense_shape] + message(24), [face_count],
                [*common, wide, send_cells],
            )
    return tuple(call(last_kernel, [(state.shape, F32)] * 2, [face_count], [*common, state]))


def solution(mesh):
    placed = (
        P(None, "inst", "dom"), P("dom"), P("dom"), P(None, "dom"), P(None, "dom"), P(None, "dom"), P("dom"), P("dom"),
        P("dom"), P("dom", None),
    )
    return jax.shard_map(
        local, mesh=mesh, in_specs=placed, out_specs=(P(None, "inst", "dom"), P(None, "inst", "dom")), check_vma=False,
    )
```

```python
import jax
import jax.numpy as jnp
import numpy as np
from jax import lax
from jax.experimental import pallas as pl
from jax.experimental.pallas import tpu as pltpu
from jax.sharding import PartitionSpec as P


HEAT_RATIO = 1.4
FREQUENCY = 0.5
NV = 5
CELLS = 512
GHOSTS = 256
FACES = 2048
CHUNK = 512
VROWS = 24
GROWS = 64
BF = jnp.bfloat16
F32 = jnp.float32


def parity_of_partition():
    return lax.axis_index("dom") & 1


def top_rows(shape):
    return (lax.broadcasted_iota(jnp.int32, shape, 0) & 7) < 4


def swap_halves(x):
    return pltpu.roll(x, 4, 0)


def fold(x):
    return x + swap_halves(x)


def split(x):
    high = x.astype(BF).astype(F32)
    return jnp.concatenate([high, x - high], axis=0).astype(BF)


def joined(x):
    rows = x.shape[0] // 2
    return x[:rows] + x[rows:]


def matmul(a, b):
    return jnp.dot(a, b, preferred_element_type=F32)


def matmul_t(a, b):
    return lax.dot_general(a, b, (((1,), (1,)), ((), ())), preferred_element_type=F32)


def one_hot(ids, rows):
    cell = lax.broadcasted_iota(jnp.int32, (rows, ids.shape[1]), 0)
    return jnp.where(cell == ids, 1.0, 0.0)


def low_lanes(shape):
    return lax.broadcasted_iota(jnp.int32, shape, 1) < 64


def listed(table, send_hot):
    packed = joined(matmul(table, send_hot))
    up, down = packed[:, :128], packed[:, 128:]
    even = parity_of_partition() == 0
    return jnp.where(even, up, down), jnp.where(even, down, up)


def dense_lists(near):
    half = near.shape[0] // 2
    turned = pltpu.roll(near[half:], 64, 1)
    low = low_lanes(turned.shape)
    first, second = jnp.where(low, near[:half], turned), jnp.where(low, turned, near[:half])
    even = parity_of_partition() == 0
    return jnp.concatenate([jnp.where(even, first, second), jnp.where(even, second, first)], axis=0)


def loose(x):
    return jnp.concatenate([x, pltpu.roll(x, 64, 1)], axis=0)


def ghost_values(near, first, second, relay):
    low = low_lanes(near.shape)
    even = parity_of_partition() == 0
    left = jnp.where(low, jnp.where(even, second, relay), jnp.where(even, first, near))
    right = jnp.where(low, jnp.where(even, near, first), jnp.where(even, relay, second))
    return split(jnp.concatenate([left, right], axis=1))


def state_ghosts(near_in, cross_in, relay_in):
    return ghost_values(near_in[...], cross_in[:VROWS], cross_in[VROWS:], relay_in[...])


def gradient_ghosts(near_in, cross_in, relay_in):
    half = GROWS // 2
    return ghost_values(loose(near_in[half:]), cross_in[:GROWS], loose(cross_in[GROWS:]), relay_in[...])


def send_kernel(
    state_hbm, send_hbm, owner_hbm, neighbor_hbm, near_ref, far_ref, dense_ref, hot_ref, owner_ref, neighbor_ref,
    state_ref, send_ref, state_sem, send_sem, owner_sem, neighbor_sem,
):
    fetch_send = pltpu.make_async_copy(send_hbm, send_ref, send_sem)
    fetch_state = pltpu.make_async_copy(state_hbm, state_ref, state_sem)
    fetch_owner = pltpu.make_async_copy(owner_hbm, owner_ref, owner_sem)
    fetch_neighbor = pltpu.make_async_copy(neighbor_hbm, neighbor_ref, neighbor_sem)
    for fetch in (fetch_send, fetch_state, fetch_owner, fetch_neighbor):
        fetch.start()
    fetch_send.wait()
    for k in range(0, 4, 2):
        pair = [one_hot(send_ref[k + j : k + j + 1, :], CELLS) for j in range(2)]
        hot_ref[:, 64 * k : 64 * k + 128] = jnp.concatenate(pair, axis=1).astype(BF)
    fetch_state.wait()
    for v in range(NV):
        dense_ref[4 * v : 4 * v + 4, :] = state_ref[v]
    dense_ref[4 * NV : VROWS, :] = state_ref[NV - 1]
    near_ref[...], far_ref[...] = listed(split(dense_ref[...]), hot_ref[...])
    fetch_owner.wait()
    fetch_neighbor.wait()


def hot_kernel(owner_ref, neighbor_ref, own_ref, other_ref):
    for f in range(0, FACES, CHUNK):
        faces = slice(f, f + CHUNK)
        own_ref[:, faces] = one_hot(owner_ref[:, faces], CELLS).astype(BF)
        other_ref[:, faces] = one_hot(neighbor_ref[:, faces], CELLS + GHOSTS).astype(BF)


def jump_kernel(dense_ref, own_ref, other_ref, jump_ref):
    values = split(dense_ref[...])
    for f in range(0, FACES, CHUNK):
        faces = slice(f, f + CHUNK)
        jump_ref[:, faces] = joined(matmul(values, other_ref[:CELLS, faces] - own_ref[:, faces]))


def gradient_kernel(
    count_ref, jump_ref, near_in, cross_in, relay_in, own_ref, other_ref, normal_ref, volume_ref, send_ref,
    table_ref, near_ref, far_ref,
):
    ghosts = state_ghosts(near_in, cross_in, relay_in)
    total = jnp.zeros((2 * GROWS, CELLS), F32)
    top = top_rows((8, CHUNK))
    for f in range(0, FACES, CHUNK):
        faces = slice(f, f + CHUNK)
        jump = jump_ref[:, faces] + joined(matmul(ghosts, other_ref[CELLS:, faces]))
        live = lax.broadcasted_iota(jnp.int32, (1, CHUNK), 1) + f < count_ref[0]
        half = [jnp.where(live, 0.5 * normal_ref[d : d + 1, faces], 0.0) for d in range(3)]
        flows = [jump[8 * j : 8 * j + 8] * half[d] for d in range(3) for j in range(2)]
        flows += [jump[16:24] * jnp.where(top, half[0], half[1]), jump[16:24] * half[2]]
        sum_hot = other_ref[:CELLS, faces] + own_ref[:, faces]
        total = total + matmul_t(split(jnp.concatenate(flows, axis=0)), sum_hot)
    table = split(joined(total) * (1.0 / volume_ref[...]))
    table_ref[...] = table
    near, far_ref[...] = listed(table, send_ref[...])
    near_ref[...] = dense_lists(near)


def with_arms(values, arm_ref, faces, top):
    state = joined(values[: 2 * VROWS])
    gradient = joined(values[2 * VROWS :])
    arms = [arm_ref[d : d + 1, faces] for d in range(3)]
    out = []
    for j in range(2):
        total = state[8 * j : 8 * j + 8]
        for d in range(3):
            total = total + gradient[16 * d + 8 * j : 16 * d + 8 * j + 8] * arms[d]
        out.append(total)
    energy = fold(gradient[48:56] * jnp.where(top, arms[0], arms[1])) + gradient[56:64] * arms[2]
    out.append(state[16:24] + energy)
    return out


def face_kernel(dense_ref, table_ref, own_ref, other_ref, owner_arm_ref, neighbor_arm_ref, face_ref):
    values = jnp.concatenate([split(dense_ref[...]), table_ref[...]], axis=0)
    top = top_rows((8, CHUNK))
    for f in range(0, FACES, CHUNK):
        faces = slice(f, f + CHUNK)
        left = with_arms(matmul(values, own_ref[:, faces]), owner_arm_ref, faces, top)
        right = with_arms(matmul(values, other_ref[:CELLS, faces]), neighbor_arm_ref, faces, top)
        for j in range(2):
            face_ref[16 * j : 16 * j + 8, faces] = jnp.where(top, left[j], swap_halves(right[j]))
            face_ref[16 * j + 8 : 16 * j + 16, faces] = jnp.where(top, swap_halves(left[j]), right[j])
        face_ref[32:40, faces] = jnp.where(top, left[2], right[2])


def spatial_part(
    count_ref, face_ref, near_in, cross_in, relay_in, gnear_in, gcross_in, grelay_in, own_ref, other_ref, normal_ref,
    neighbor_arm_ref, volume_ref,
):
    ghosts = state_ghosts(near_in, cross_in, relay_in)
    values = jnp.concatenate([ghosts, gradient_ghosts(gnear_in, gcross_in, grelay_in)], axis=0)
    total = jnp.zeros((2 * VROWS, CELLS), F32)
    top = top_rows((8, CHUNK))
    sign = jnp.where(top, 1.0, -1.0)
    for f in range(0, FACES, CHUNK):
        faces = slice(f, f + CHUNK)
        right = with_arms(matmul(values, other_ref[CELLS:, faces]), neighbor_arm_ref, faces, top)
        bottom = [swap_halves(right[0]), right[0], swap_halves(right[1]), right[1], right[2]]
        states = [face_ref[8 * v : 8 * v + 8, faces] + jnp.where(top, 0.0, bottom[v]) for v in range(NV)]
        live = lax.broadcasted_iota(jnp.int32, (1, CHUNK), 1) + f < count_ref[0]
        normals = [jnp.where(live, normal_ref[d : d + 1, faces], 0.0) for d in range(3)]
        area = jnp.sqrt(normals[0] * normals[0] + normals[1] * normals[1] + normals[2] * normals[2])
        density, energy = states[0], states[4]
        momentum = states[1:4]
        inverse = 1.0 / density
        velocity = [m * inverse for m in momentum]
        kinetic = momentum[0] * velocity[0] + momentum[1] * velocity[1] + momentum[2] * velocity[2]
        pressure = (HEAT_RATIO - 1.0) * (energy - 0.5 * kinetic)
        speed = velocity[0] * normals[0] + velocity[1] * normals[1] + velocity[2] * normals[2]
        wave = jnp.abs(speed) + jnp.sqrt(HEAT_RATIO * pressure * inverse) * area
        wave = jnp.maximum(wave, swap_halves(wave)) * sign
        flux = [density * speed]
        for d in range(3):
            flux.append(momentum[d] * speed + pressure * normals[d])
        flux.append((energy + pressure) * speed)
        twice = [flux[v] + wave * states[v] for v in range(NV)]
        sums = []
        for j in range(2):
            a, b = twice[2 * j], twice[2 * j + 1]
            sums.append(jnp.where(top, a, b) + swap_halves(jnp.where(top, b, a)))
        sums.append(fold(twice[4]))
        difference = own_ref[:, faces] - other_ref[:CELLS, faces]
        total = total + matmul_t(split(jnp.concatenate(sums, axis=0)), difference)
    return joined(total) * (0.5 / volume_ref[...])


def middle_kernel(*refs):
    *common, spectral_ref, step_ref, dense_ref, send_ref, dense_out, near_ref, far_ref = refs
    rate = spatial_part(*common) + spectral_ref[...]
    dense = dense_ref[...] - 0.5 * step_ref[...] * rate
    dense_out[...] = dense
    near_ref[...], far_ref[...] = listed(split(dense), send_ref[...])


def last_kernel(*refs):
    *common, spectral_ref, step_ref, state_ref, new_ref, residual_ref = refs
    rate = spatial_part(*common) + spectral_ref[...]
    for v in range(NV):
        rows = rate[4 * v : 4 * v + 4]
        residual_ref[v] = rows
        new_ref[v] = state_ref[v] - step_ref[...] * rows


def spectral_kernel(matrix_ref, mine_ref, next_ref, rest_ref, out_ref):
    matrix = matrix_ref[lax.axis_index("inst")]
    data = jnp.concatenate([mine_ref[...], next_ref[...], rest_ref[...]], axis=0)
    m_high, d_high = matrix.astype(BF), data.astype(BF)
    m_low, d_low = (matrix - m_high.astype(F32)).astype(BF), (data - d_high.astype(F32)).astype(BF)
    out_ref[...] = matmul(m_high, d_high) + matmul(m_high, d_low) + matmul(m_low, d_high)


def spectral_matrices(groups, size):
    points = groups * size
    distance = np.arange(points)[:, None] - np.arange(points)[None, :]
    safe = np.where(distance == 0, 1, distance)
    table = 0.5 * np.where(distance % 2 == 0, 1.0, -1.0) / np.tan(np.pi * safe / points)
    table = np.where(distance == 0, 0.0, table) * FREQUENCY
    out = np.zeros((groups, VROWS, groups * VROWS), np.float32)
    for y in range(groups):
        for row in range(VROWS):
            variable, instance = min(row // size, NV - 1), row % size
            for b in range(groups):
                for t in range(size):
                    column = b * VROWS + size * variable + t
                    out[y, row, column] = table[size * y + instance, size * (y ^ (0, 1, 3, 2)[b]) + t]
    return out


def call(kernel, outputs, scalars, arrays, hbm=0, scratch=(), limit=8):
    smem = pl.BlockSpec(memory_space=pltpu.SMEM)
    vmem = pl.BlockSpec(memory_space=pltpu.VMEM)
    far = pl.BlockSpec(memory_space=pltpu.HBM)
    return pl.pallas_call(
        kernel,
        out_shape=[jax.ShapeDtypeStruct(s, d) for s, d in outputs],
        in_specs=[smem] * len(scalars) + [far] * hbm + [vmem] * (len(arrays) - hbm),
        out_specs=[vmem] * len(outputs),
        scratch_shapes=scratch,
        compiler_params=pltpu.CompilerParams(vmem_limit_bytes=limit << 20),
    )(*scalars, *arrays)


def local(
    state, cell_volume, step_size, face_normal, owner_arm, neighbor_arm, face_owner, face_neighbor, face_count,
    send_cells,
):
    parts = lax.axis_size("dom")
    volume = cell_volume.reshape(1, CELLS)
    step = step_size.reshape(1, CELLS)
    owner = face_owner.reshape(1, FACES)
    neighbor = face_neighbor.reshape(1, FACES)
    matrices = jnp.asarray(spectral_matrices(lax.axis_size("inst"), state.shape[1]))
    inside = [(i, i ^ 1) for i in range(parts)]
    lines = lax.axis_size("inst")
    across = []
    for i in range(parts):
        for y in range(lines):
            j = i + 1 if i % 2 else i - 1
            across.append((lines * i + y, lines * j + y if 0 <= j < parts else lines * i + (y ^ 1)))

    def exchange(near, far, forwarded):
        got = lax.ppermute(near, "dom", inside)
        outgoing = jnp.concatenate([far, got[:forwarded]], axis=0)
        cross = lax.ppermute(outgoing, ("dom", "inst"), across)
        relay = lax.ppermute(cross[: far.shape[0]], "dom", inside)
        return got, cross, relay

    def instances(dense):
        one = lax.ppermute(dense, "inst", [(i, i ^ 1) for i in range(4)])
        outgoing = jnp.concatenate([dense, one], axis=0)
        rest = lax.ppermute(outgoing, "inst", [(i, i ^ 3) for i in range(4)])
        arrays = [matrices, dense, one, rest]
        return call(spectral_kernel, [((VROWS, CELLS), F32)], [], arrays)[0]

    def message(rows):
        return [((rows, 128), F32)] * 2

    dense_shape = ((VROWS, CELLS), F32)
    sources = [pltpu.with_memory_space_constraint(x, pltpu.HBM) for x in (state, send_cells, owner, neighbor)]
    ids = ((1, FACES), jnp.int32)
    near, far, dense, send_hot, owner, neighbor = call(
        send_kernel, message(VROWS) + [dense_shape, ((CELLS, GHOSTS), BF), ids, ids], [], sources, hbm=4,
        scratch=[pltpu.VMEM(state.shape, F32), pltpu.VMEM(send_cells.shape, jnp.int32)] + [pltpu.SemaphoreType.DMA] * 4,
    )
    hot = call(hot_kernel, [((CELLS, FACES), BF), ((CELLS + GHOSTS, FACES), BF)], [], [owner, neighbor])
    for section in range(2):
        jump = call(jump_kernel, [((VROWS, FACES), F32)], [], [dense, *hot])[0]
        ghosts = exchange(near, far, VROWS)
        spectral = instances(dense)
        table, gnear, gfar = call(
            gradient_kernel, [((2 * GROWS, CELLS), BF)] + message(GROWS), [face_count],
            [jump, *ghosts, *hot, face_normal, volume, send_hot],
        )
        arrays = [dense, table, *hot, owner_arm, neighbor_arm]
        face = call(face_kernel, [((8 * NV, FACES), F32)], [], arrays)[0]
        gradient_blocks = exchange(gnear, gfar, GROWS // 2)
        common = [face, *ghosts, *gradient_blocks, *hot, face_normal, neighbor_arm, volume, spectral, step]
        if section == 0:
            dense, near, far = call(
                middle_kernel, [dense_shape] + message(VROWS), [face_count], [*common, dense, send_hot]
            )
    return tuple(call(last_kernel, [(state.shape, F32)] * 2, [face_count], [*common, state]))


def solution(mesh):
    placed = (
        P(None, "inst", "dom"), P("dom"), P("dom"), P(None, "dom"), P(None, "dom"), P(None, "dom"), P("dom"), P("dom"),
        P("dom"), P("dom", None),
    )
    return jax.shard_map(
        local, mesh=mesh, in_specs=placed, out_specs=(P(None, "inst", "dom"), P(None, "inst", "dom")), check_vma=False,
    )
```
